32 devices in a mesh: gx: 4 (over z), gy: 2 (over y), gz: 4 (over x, core).
Axes of the slice: x: 2, y: 2, z: 4, core: 2. Of those that a mesh axis runs over, the one named last changes fastest.
Arguments:
- scalar_field: float32 [32, 64, 2048], P('gx', 'gy', 'gz'), may hold values from -6 to 6
- velocity: float32 [3, 32, 64, 2048], P(None, 'gx', 'gy', 'gz'), may hold values from -2.5 to 2.5
- reaction_rate: float32 [32, 64, 2048], P('gx', 'gy', 'gz'), may hold values from 0.3 to 3
- sample_cells: int32 [4, 2, 512], P('gx', 'gy', 'gz'), may hold values from 0 to 255
- weight_in: bfloat16 [3072, 1024], P(('gx', 'gy', 'gz')), may hold values from -0.1875 to 0.1875
- weight_out: bfloat16 [3072, 512], P(('gx', 'gy', 'gz')), may hold values from -0.109375 to 0.109375
Outputs:
- advanced: float32 [32, 64, 2048], P('gx', 'gy', 'gz')
- grad_in: float32 [3072, 1024], P(('gx', 'gy', 'gz'))
- grad_out: float32 [3072, 512], P(('gx', 'gy', 'gz'))
The draws below stay inside these ranges and needn't reach their ends.
All inputs are finite; a program needn't handle non-finite values.
Results may differ from the reference program's by a relative error of at most 0.0011.
Values may be sent and summed in bfloat16 or wider, within the bound.
A program may use at most 64 MiB of HBM per device.

```python
import math
import jax
import jax.numpy as jnp
from jax import lax

CX = 8
CY = 32
PEN = 512
IN = 1024
HID = 3072
S_DEV = 128
STEPS = 3
SAMPLES = 4096
NX = 32
NY = 64
NZ = 2048
N_GX = 4
N_GY = 2
N_GZ = 4


def with_ends(values, key, smallest, high):
    place = [jax.random.randint(jax.random.fold_in(key, axis), (), 0, length) for axis, length in enumerate(values.shape)]
    main_axis = values.shape.index(max(values.shape))
    neighbour = place[:main_axis] + [(place[main_axis] + 1) % values.shape[main_axis]] + place[main_axis + 1:]
    return values.at[tuple(place)].set(smallest).at[tuple(neighbour)].set(high)


def block_levels(rng, shape, pieces, least, top_value):
    def one(axis_at, blocks):
        heights = jax.random.uniform(jax.random.fold_in(jax.random.fold_in(rng, 6), axis_at), (blocks,), jnp.float32, least / len(pieces), top_value / len(pieces))
        return jnp.repeat(jnp.exp(heights), shape[axis_at] // blocks).reshape((-1,) + (1,) * (len(shape) - axis_at - 1))

    factor_of = one(*pieces[0])
    for cut in pieces[1:]:
        factor_of = factor_of * one(*cut)
    return factor_of


def normal_values(stream_key, shape, spread, limit, cuts=(), held_as=jnp.bfloat16):
    result = jax.random.normal(stream_key, shape, jnp.float32) * spread
    if len(cuts) > 0:
        result = block_levels(stream_key, shape, cuts, -0.22, 0.18) * result
    return jnp.clip(result, min=-limit, max=limit).astype(held_as)


def setup_inputs(seed: int = 0) -> dict:
    streams_of = jax.random.split(jax.random.key(seed), 7)
    return {
        "scalar_field": normal_values(streams_of[0], (NX, NY, NZ), 1.0, 6.0, ((0, 4), (1, 2), (2, 4)), jnp.float32),
        "velocity": normal_values(streams_of[1], (3, NX, NY, NZ), 0.4, 2.5, ((1, 4), (2, 2), (3, 4)), jnp.float32),
        "reaction_rate": jnp.clip(jnp.exp(math.log(3.0) - 2.3025851 * jax.random.uniform(streams_of[2], (NX, NY, NZ), jnp.float32) ** block_levels(streams_of[2], (NX, NY, NZ), ((0, 4), (1, 2), (2, 4)), -0.2, 0.2)), 0.3, 3.0),
        "sample_cells": with_ends(jax.random.randint(streams_of[3], (N_GX, N_GY, N_GZ * S_DEV), 0, CX * CY), jax.random.fold_in(streams_of[3], 1), 0, (CX * CY) - 1).astype(jnp.int32),
        "weight_in": normal_values(streams_of[4], (HID, IN), IN ** -0.5, 0.1875, ((0, 32),)),
        "weight_out": normal_values(streams_of[5], (HID, PEN), HID ** -0.5, 0.109375, ((0, 32),)),
    }


TIME_STEP = 0.15


def update(field, velocity, reaction_rate):
    x_plus = jnp.roll(field, -1, 0)
    x_minus = jnp.roll(field, 1, 0)
    y_plus = jnp.roll(field, -1, 1)
    y_minus = jnp.roll(field, 1, 1)
    z_plus = jnp.roll(field, -1, 2)
    z_minus = jnp.roll(field, 1, 2)
    laplace = (x_plus + x_minus) + (y_plus + y_minus) + (z_plus + z_minus) - 6.0 * field
    advect = velocity[0] * (x_plus - x_minus) + velocity[1] * (y_plus - y_minus) + velocity[2] * (z_plus - z_minus)
    return field + TIME_STEP * (laplace - 0.5 * advect - reaction_rate * field)


def dsilu(value):
    sig = jax.nn.sigmoid(value)
    return sig * (1.0 + value * (1.0 - sig))


def blocks_of(field):
    shaped = field.reshape(N_GX, CX, N_GY, CY, N_GZ, PEN)
    return shaped.transpose(0, 2, 4, 1, 3, 5).reshape(N_GX * N_GY * N_GZ, CX * CY, PEN)


def reference(scalar_field, velocity, reaction_rate, sample_cells, weight_in, weight_out):
    snaps = []
    current = scalar_field
    for step_num in range(STEPS):
        current = update(current, velocity, reaction_rate)
        snaps.append(current)
    first = blocks_of(snaps[0])
    second = blocks_of(snaps[1])
    third = blocks_of(snaps[2])
    picks = sample_cells.reshape(N_GX, N_GY, N_GZ, S_DEV).reshape(N_GX * N_GY * N_GZ, S_DEV).astype(jnp.int32)
    scale = 1.0 / (float(SAMPLES) ** 0.5)
    contract_last = (((1,), (1,)), ((), ()))
    contract_first = (((0,), (0,)), ((), ()))

    def one_block(carry, block):
        first_b, second_b, third_b, pick_b = block
        inputs = jnp.concatenate([jnp.take(first_b, pick_b, axis=0), jnp.take(second_b, pick_b, axis=0)], 1).astype(jnp.bfloat16)
        target = jnp.take(third_b, pick_b, axis=0)
        preact = lax.dot_general(inputs, weight_in, contract_last, preferred_element_type=jnp.float32)
        hidden = jax.nn.silu(preact).astype(jnp.bfloat16)
        predict = jnp.dot(hidden, weight_out, preferred_element_type=jnp.float32)
        resid = ((predict - target) * scale).astype(jnp.bfloat16)
        back = lax.dot_general(resid, weight_out, contract_last, preferred_element_type=jnp.float32)
        dpre = (back * dsilu(preact)).astype(jnp.bfloat16)
        g_in = carry[0] + lax.dot_general(dpre, inputs, contract_first, preferred_element_type=jnp.float32)
        g_out = carry[1] + lax.dot_general(hidden, resid, contract_first, preferred_element_type=jnp.float32)
        return (g_in, g_out), None

    start = (jnp.zeros((HID, IN), jnp.float32), jnp.zeros((HID, PEN), jnp.float32))
    (grad_in, grad_out), unused = lax.scan(one_block, start, (first, second, third, picks))
    return snaps[2], grad_in, grad_out
```

```python
import functools
import math

import jax
import jax.numpy as jnp
from jax import lax
from jax.experimental import pallas as pl
from jax.experimental.pallas import tpu as pltpu
from jax.sharding import PartitionSpec as P

STEPS = 3
TIME_STEP = 0.15
SPLIT = 2
NT = (((1,), (1,)), ((), ()))
TN = (((0,), (0,)), ((), ()))
F32 = jnp.float32
BF16 = jnp.bfloat16


def mm(a, b, dims=None):
    if dims is None:
        return jnp.dot(a, b, preferred_element_type=F32)
    return lax.dot_general(a, b, dims, preferred_element_type=F32)


def dsilu(value):
    sig = 1.0 / (1.0 + jnp.exp(-value))
    return sig * (1.0 + value * (1.0 - sig))


def log2(n):
    bits = n.bit_length() - 1
    assert 1 << bits == n
    return bits


def kernel(
    sizes, scale,
    u_ref, vel_ref, rate_ref, picks_ref, win_ref, wout_ref,
    adv_ref, gin_ref, gout_ref,
    snaps, hx, hy_out, hy, hz, xin, win, wout, pre, hid, part, prv, res, g, rbuf,
    halo_s, halo_r, x_s, x_r, w_s, w_r, p_s, p_r, q_s, q_r, g_s, g_r, loc,
):
    T, NY, NZ = sizes
    D = NY * NZ
    nb, nzb = log2(D), log2(NZ)
    gx, gy, gz = lax.axis_index("gx"), lax.axis_index("gy"), lax.axis_index("gz")
    me = gy * NZ + gz
    mb = [(me // (1 << b)) % 2 for b in range(nb)]
    CX, CY, PEN = adv_ref.shape
    S = picks_ref.shape[1]
    Hc = win_ref.shape[0]
    IN = win_ref.shape[1]
    NS = g.shape[0]
    W = g.shape[3]

    def partner(b):
        if b < nzb:
            return {"gz": gz + (1 - 2 * mb[b]) * (1 << b)}
        return {"gy": gy + (1 - 2 * mb[b]) * (1 << (b - nzb))}

    peers = [{"gx": (gx + k) % T} for k in range(1, T)]
    sides = [
        ({"gx": (gx + 1) % T}, {"gx": (gx + T - 1) % T}),
        ({"gy": (gy + 1) % NY}, {"gy": (gy + NY - 1) % NY}),
        ({"gz": (gz + 1) % NZ}, {"gz": (gz + NZ - 1) % NZ}),
    ]

    def remote(src, dst, ss, rs, dev):
        return pltpu.make_async_remote_copy(
            src_ref=src, dst_ref=dst, send_sem=ss, recv_sem=rs,
            device_id=dev, device_id_type=pl.DeviceIdType.MESH,
        )

    own_in = pltpu.make_async_copy(win_ref, win.at[me], loc.at[0])
    own_out = pltpu.make_async_copy(wout_ref, wout.at[me], loc.at[1])
    first = pltpu.make_async_copy(u_ref, snaps.at[0], loc.at[2])
    own_in.start()
    own_out.start()
    first.start()

    barrier = pltpu.get_barrier_semaphore()
    greet = peers + [partner(b) for b in range(nb)] + list(sides[1]) + list(sides[2])
    for dev in greet:
        pl.semaphore_signal(barrier, inc=1, device_id=dev, device_id_type=pl.DeviceIdType.MESH)
    pl.semaphore_wait(barrier, len(greet))
    first.wait()

    w_bufs = ((win, list(range(nb - 1, -1, -1))), (wout, list(range(1, nb)) + [0]))

    def w_copies(stream, stage):
        buf, order = w_bufs[stream]
        done, cur = order[:stage], order[stage]
        out = []
        for k in range(1 << stage):
            c = sum(mb[b] * (1 << b) for b in range(nb) if b not in done)
            c = c + sum(((k >> j) & 1) * (1 << b) for j, b in enumerate(done))
            theirs = c + (1 - 2 * mb[cur]) * (1 << cur)
            slot = (1 << stage) - 1 + k
            sems = (w_s.at[stream, slot], w_r.at[stream, slot])
            send = remote(buf.at[c], buf.at[c], *sems, partner(cur))
            recv = remote(buf.at[theirs], buf.at[theirs], *sems, partner(cur))
            out.append((send, recv))
        return out

    def w_start(stage):
        for stream in range(2):
            for send, _ in w_copies(stream, stage):
                send.start()

    def w_wait(stage):
        for stream in range(2):
            for _, recv in w_copies(stream, stage):
                recv.wait_recv()

    def halo(step):
        cur = snaps.at[step]
        rows = CX * CY
        faces = [
            (cur.at[pl.ds(rows - CY, CY)], hx.at[step, 0], sides[0][0]),
            (cur.at[pl.ds(0, CY)], hx.at[step, 1], sides[0][1]),
            (hy_out.at[step, 0], hy.at[step, 0], sides[1][0]),
            (hy_out.at[step, 1], hy.at[step, 1], sides[1][1]),
            (cur.at[:, pl.ds(PEN - 128, 128)], hz.at[step, 0], sides[2][0]),
            (cur.at[:, pl.ds(0, 128)], hz.at[step, 1], sides[2][1]),
        ]
        return [
            remote(s, d, halo_s.at[step, i], halo_r.at[step, i], dev)
            for i, (s, d, dev) in enumerate(faces)
        ]

    def halo_start(step):
        copies = halo(step)
        for i in (0, 1, 4, 5):
            copies[i].start()
        for i in range(CX):
            hy_out[step, 0, pl.ds(i, 1), :] = snaps[step, pl.ds(i * CY + CY - 1, 1), :]
            hy_out[step, 1, pl.ds(i, 1), :] = snaps[step, pl.ds(i * CY, 1), :]
        copies[2].start()
        copies[3].start()

    row_id = lax.broadcasted_iota(jnp.int32, (CY, PEN), 0)
    lane_id = lax.broadcasted_iota(jnp.int32, (CY, PEN), 1)

    def advance(step):
        for c in halo(step):
            c.wait_recv()

        def layer(i):
            if i < 0:
                return hx[step, 0]
            if i >= CX:
                return hx[step, 1]
            return snaps[step, pl.ds(i * CY, CY), :]

        for i in range(CX):
            u = layer(i)
            xp, xm = layer(i + 1), layer(i - 1)
            yp = jnp.where(row_id == CY - 1, hy[step, 1, pl.ds(i, 1), :], pltpu.roll(u, CY - 1, 0))
            ym = jnp.where(row_id == 0, hy[step, 0, pl.ds(i, 1), :], pltpu.roll(u, 1, 0))
            zhi = hz[step, 1, pl.ds(i * CY, CY), :][:, 0:1]
            zlo = hz[step, 0, pl.ds(i * CY, CY), :][:, 127:128]
            zp = jnp.where(lane_id == PEN - 1, zhi, pltpu.roll(u, PEN - 1, 1))
            zm = jnp.where(lane_id == 0, zlo, pltpu.roll(u, 1, 1))
            lap = (xp + xm) + (yp + ym) + (zp + zm) - 6.0 * u
            adv = vel_ref[0, i] * (xp - xm) + vel_ref[1, i] * (yp - ym) + vel_ref[2, i] * (zp - zm)
            new = u + TIME_STEP * (lap - 0.5 * adv - rate_ref[i] * u)
            if step == STEPS - 1:
                adv_ref[i] = new
            else:
                snaps[step + 1, pl.ds(i * CY, CY), :] = new

    hot = jnp.where(
        lax.broadcasted_iota(jnp.int32, (CX * CY, S), 0) == picks_ref[...], 1.0, 0.0
    ).astype(BF16)

    def x_copies(half):
        cols = pl.ds(half * PEN, PEN)
        return [
            (
                remote(xin.at[gx, :, cols], xin.at[gx, :, cols], x_s.at[half, k], x_r.at[half, k], dev),
                remote(
                    xin.at[(gx + T - 1 - k) % T, :, cols], xin.at[(gx + T - 1 - k) % T, :, cols],
                    x_s.at[half, k], x_r.at[half, k], dev,
                ),
            )
            for k, dev in enumerate(peers)
        ]

    def x_send(half):
        xin[gx, :, pl.ds(half * PEN, PEN)] = mm(hot, snaps[half + 1].astype(BF16), TN).astype(BF16)
        for send, _ in x_copies(half):
            send.start()

    halo_start(0)
    own_in.wait()
    own_out.wait()
    w_start(0)
    w_stage = 0
    for step in range(STEPS):
        advance(step)
        if step < STEPS - 1:
            halo_start(step + 1)
            x_send(step)
        if w_stage < nb - 1:
            w_wait(w_stage)
            w_stage += 1
            w_start(w_stage)
    snap3 = adv_ref[...].reshape(CX * CY, PEN)
    hi = snap3.astype(BF16)
    rest = snap3 - hi.astype(F32)
    mid = rest.astype(BF16)
    low = (rest - mid.astype(F32)).astype(BF16)
    target = (mm(hot, hi, TN) + mm(hot, mid, TN)) + mm(hot, low, TN)
    while True:
        w_wait(w_stage)
        w_stage += 1
        if w_stage == nb:
            break
        w_start(w_stage)
    for half in range(2):
        for _, recv in x_copies(half):
            recv.wait_recv()

    cb = 4 if D % 4 == 0 else D
    SA = T * S

    @pl.loop(0, D // cb)
    def _(b):
        rows = pl.ds(b * cb, cb)
        v = mm(win[rows].reshape(cb * Hc, IN), xin[...].reshape(SA, IN), NT)
        pre[rows] = v.reshape(cb, Hc, SA)
        hid[rows] = (v / (1.0 + jnp.exp(-v))).astype(BF16).reshape(cb, Hc, SA)

    def predict(t):
        h = hid[:, :, pl.ds(pl.multiple_of(t * S, S), S)].reshape(D * Hc, S)
        return mm(h, wout[...].reshape(D * Hc, PEN), TN)

    p_copies = [
        remote(part.at[k], prv.at[k], p_s.at[k], p_r.at[k], dev) for k, dev in enumerate(peers)
    ]
    for k in range(T - 1):
        part[k] = predict((gx + 1 + k) % T)
        p_copies[k].start()
    total = predict(gx)
    for k in range(T - 1):
        p_copies[k].wait_recv()
        total = total + prv[k]
    res[gx] = ((total - target) * scale).astype(BF16)
    q_copies = []
    for k, dev in enumerate(peers):
        src = (gx + T - 1 - k) % T
        send = remote(res.at[gx], res.at[gx], q_s.at[k], q_r.at[k], dev)
        recv = remote(res.at[src], res.at[src], q_s.at[k], q_r.at[k], dev)
        send.start()
        q_copies.append((send, recv))
    for _, recv in q_copies:
        recv.wait_recv()

    orders = [[0] + list(range(1, nb)), [0] + list(range(nb - 1, 0, -1))]
    offs = [sum(D >> (j + 1) for j in range(s)) for s in range(nb)]

    def g_slot(stage, vals):
        return offs[stage] + sum(v * (1 << j) for j, v in enumerate(vals))

    def g_copy(stream, stage, vals):
        order = orders[stream % 2]
        cur = order[stage]
        c = sum(mb[b] * (1 << b) for b in order[:stage]) + (1 - mb[cur]) * (1 << cur)
        c = c + sum(v * (1 << b) for v, b in zip(vals, order[stage + 1:]))
        slot = g_slot(stage, vals)
        keep = c + (2 * mb[cur] - 1) * (1 << cur)
        copy = remote(
            g.at[stream, c], rbuf.at[stream, slot], g_s.at[stream, slot], g_r.at[stream, slot],
            partner(cur),
        )
        return copy, slot, keep

    def patterns(n):
        return [[(k >> j) & 1 for j in range(n)] for k in range(1 << n)]

    for b in range(D // cb):
        rows = pl.ds(b * cb, cb)
        allres = res[...].reshape(SA, PEN)
        back = mm(wout[rows].reshape(cb * Hc, PEN), allres, NT)
        dpre = (back * dsilu(pre[rows].reshape(cb * Hc, SA))).astype(BF16)
        h = hid[rows].reshape(cb * Hc, SA)
        for stream in range(NS):
            if stream < IN // W:
                x = xin[:, :, pl.ds(stream * W, W)].reshape(SA, W)
                val = mm(dpre, x)
            else:
                val = mm(h, res[:, :, pl.ds(stream * W - IN, W)].reshape(SA, W))
            g[stream, rows] = val.reshape(cb, Hc, W)
            rest_bits = orders[stream % 2][1:]
            for vals in patterns(nb - 1):
                low_c = sum(v * (1 << bb) for v, bb in zip(vals, rest_bits))
                if b * cb <= low_c < (b + 1) * cb:
                    g_copy(stream, 0, vals)[0].start()
    for stage in range(nb):
        for stream in range(NS):
            order = orders[stream % 2]
            n = nb - 1 - stage
            if n == 0:
                copy, slot, keep = g_copy(stream, stage, [])
                copy.wait_recv()
                val = g[stream, keep] + rbuf[stream, slot]
                if stream < IN // W:
                    gin_ref[:, pl.ds(stream * W, W)] = val
                else:
                    gout_ref[:, pl.ds(stream * W - IN, W)] = val
                continue
            nxt = mb[order[stage + 1]]
            for flip in (1, 0):
                bit = 1 - nxt if flip else nxt
                for vals in patterns(n - 1):
                    copy, slot, keep = g_copy(stream, stage, [bit] + vals)
                    copy.wait_recv()
                    g[stream, keep] = g[stream, keep] + rbuf[stream, slot]
                    if flip:
                        g_copy(stream, stage + 1, vals)[0].start()

    for step in range(STEPS):
        for c in halo(step):
            c.wait_send()
    for stream in range(2):
        for stage in range(nb):
            for send, _ in w_copies(stream, stage):
                send.wait_send()
    for half in range(2):
        for send, _ in x_copies(half):
            send.wait_send()
    for k in range(T - 1):
        p_copies[k].wait_send()
        q_copies[k][0].wait_send()
    for stream in range(NS):
        for stage in range(nb):
            for vals in patterns(nb - 1 - stage):
                g_copy(stream, stage, vals)[0].wait_send()


def shards(sizes, scalar_field, velocity, reaction_rate, sample_cells, weight_in, weight_out):
    T, NY, NZ = sizes
    D = NY * NZ
    nb = log2(D)
    CX, CY, PEN = scalar_field.shape
    S = sample_cells.shape[-1]
    Hc, IN = weight_in.shape
    SA = T * S
    W = PEN // SPLIT
    NS = (IN + PEN) // W
    scale = 1.0 / math.sqrt(S * T * D)
    rows = CX * CY
    dma = pltpu.SemaphoreType.DMA
    vmem = pl.BlockSpec(memory_space=pltpu.VMEM)
    return tuple(pl.pallas_call(
        functools.partial(kernel, sizes, scale),
        out_shape=(
            jax.ShapeDtypeStruct((CX, CY, PEN), F32),
            jax.ShapeDtypeStruct((Hc, IN), F32),
            jax.ShapeDtypeStruct((Hc, PEN), F32),
        ),
        in_specs=[vmem] * 6,
        out_specs=(vmem,) * 3,
        scratch_shapes=[
            pltpu.VMEM((STEPS, rows, PEN), F32),
            pltpu.VMEM((STEPS, 2, CY, PEN), F32),
            pltpu.VMEM((STEPS, 2, CX, PEN), F32),
            pltpu.VMEM((STEPS, 2, CX, PEN), F32),
            pltpu.VMEM((STEPS, 2, rows, 128), F32),
            pltpu.VMEM((T, S, IN), BF16),
            pltpu.VMEM((D, Hc, IN), BF16),
            pltpu.VMEM((D, Hc, PEN), BF16),
            pltpu.VMEM((D, Hc, SA), F32),
            pltpu.VMEM((D, Hc, SA), BF16),
            pltpu.VMEM((T - 1, S, PEN), F32),
            pltpu.VMEM((T - 1, S, PEN), F32),
            pltpu.VMEM((T, S, PEN), BF16),
            pltpu.VMEM((NS, D, Hc, W), F32),
            pltpu.VMEM((NS, D - 1, Hc, W), F32),
            dma((STEPS, 6)), dma((STEPS, 6)),
            dma((2, T - 1)), dma((2, T - 1)),
            dma((2, D - 1)), dma((2, D - 1)),
            dma((T - 1,)), dma((T - 1,)),
            dma((T - 1,)), dma((T - 1,)),
            dma((NS, D - 1)), dma((NS, D - 1)),
            dma((3,)),
        ],
        compiler_params=pltpu.CompilerParams(
            collective_id=0, has_side_effects=True, vmem_limit_bytes=60 * 1024 * 1024
        ),
    )(
        scalar_field.reshape(rows, PEN), velocity, reaction_rate,
        sample_cells.reshape(1, S), weight_in, weight_out,
    ))


def solution(mesh):
    sizes = (mesh.shape["gx"], mesh.shape["gy"], mesh.shape["gz"])
    in_specs = (
        P("gx", "gy", "gz"),
        P(None, "gx", "gy", "gz"),
        P("gx", "gy", "gz"),
        P("gx", "gy", "gz"),
        P(("gx", "gy", "gz"), None),
        P(("gx", "gy", "gz"), None),
    )
    out_specs = (P("gx", "gy", "gz"), P(("gx", "gy", "gz"), None), P(("gx", "gy", "gz"), None))
    return jax.shard_map(
        functools.partial(shards, sizes), mesh=mesh, in_specs=in_specs, out_specs=out_specs,
        check_vma=False,
    )
```

```python
import functools
import math

import jax
import jax.numpy as jnp
from jax import lax
from jax.experimental import pallas as pl
from jax.experimental.pallas import tpu as pltpu
from jax.sharding import PartitionSpec as P

STEPS = 3
TIME_STEP = 0.15
SPLIT = 2
NT = (((1,), (1,)), ((), ()))
TN = (((0,), (0,)), ((), ()))
F32 = jnp.float32
BF16 = jnp.bfloat16


def mm(a, b, dims=None):
    if dims is None:
        return jnp.dot(a, b, preferred_element_type=F32)
    return lax.dot_general(a, b, dims, preferred_element_type=F32)


def dsilu(value):
    sig = 1.0 / (1.0 + jnp.exp(-value))
    return sig * (1.0 + value * (1.0 - sig))


def log2(n):
    bits = n.bit_length() - 1
    assert 1 << bits == n
    return bits


def kernel(
    sizes, scale,
    u_ref, vel_ref, rate_ref, picks_ref, win_ref, wout_ref,
    adv_ref, gin_ref, gout_ref,
    snaps, hx, hy_out, hy, hz, xin, win, wout, pre, hid, part, prv, res, g, rbuf,
    halo_s, halo_r, x_s, x_r, w_s, w_r, p_s, p_r, q_s, q_r, g_s, g_r, loc,
):
    T, NY, NZ = sizes
    D = NY * NZ
    nb, nzb = log2(D), log2(NZ)
    gx, gy, gz = lax.axis_index("gx"), lax.axis_index("gy"), lax.axis_index("gz")
    me = gy * NZ + gz
    mb = [(me // (1 << b)) % 2 for b in range(nb)]
    CX, CY, PEN = adv_ref.shape
    S = picks_ref.shape[1]
    Hc = win_ref.shape[0]
    IN = win_ref.shape[1]
    NS = g.shape[0]
    W = g.shape[3]

    def partner(b):
        if b < nzb:
            return {"gz": gz + (1 - 2 * mb[b]) * (1 << b)}
        return {"gy": gy + (1 - 2 * mb[b]) * (1 << (b - nzb))}

    peers = [{"gx": (gx + k) % T} for k in range(1, T)]
    sides = [
        ({"gx": (gx + 1) % T}, {"gx": (gx + T - 1) % T}),
        ({"gy": (gy + 1) % NY}, {"gy": (gy + NY - 1) % NY}),
        ({"gz": (gz + 1) % NZ}, {"gz": (gz + NZ - 1) % NZ}),
    ]

    def remote(src, dst, ss, rs, dev):
        return pltpu.make_async_remote_copy(
            src_ref=src, dst_ref=dst, send_sem=ss, recv_sem=rs,
            device_id=dev, device_id_type=pl.DeviceIdType.MESH,
        )

    own_in = pltpu.make_async_copy(win_ref, win.at[me], loc.at[0])
    own_out = pltpu.make_async_copy(wout_ref, wout.at[me], loc.at[1])
    first = pltpu.make_async_copy(u_ref, snaps.at[0], loc.at[2])
    own_in.start()
    own_out.start()
    first.start()

    barrier = pltpu.get_barrier_semaphore()
    greet = peers + [partner(b) for b in range(nb)] + list(sides[1]) + list(sides[2])
    for dev in greet:
        pl.semaphore_signal(barrier, inc=1, device_id=dev, device_id_type=pl.DeviceIdType.MESH)
    pl.semaphore_wait(barrier, len(greet))
    first.wait()

    w_bufs = ((win, list(range(nb - 1, -1, -1))), (wout, list(range(1, nb)) + [0]))

    def w_copies(stream, stage):
        buf, order = w_bufs[stream]
        done, cur = order[:stage], order[stage]
        out = []
        for k in range(1 << stage):
            c = sum(mb[b] * (1 << b) for b in range(nb) if b not in done)
            c = c + sum(((k >> j) & 1) * (1 << b) for j, b in enumerate(done))
            theirs = c + (1 - 2 * mb[cur]) * (1 << cur)
            slot = (1 << stage) - 1 + k
            sems = (w_s.at[stream, slot], w_r.at[stream, slot])
            send = remote(buf.at[c], buf.at[c], *sems, partner(cur))
            recv = remote(buf.at[theirs], buf.at[theirs], *sems, partner(cur))
            out.append((send, recv))
        return out

    def w_start(stage):
        for stream in range(2):
            for send, _ in w_copies(stream, stage):
                send.start()

    def w_wait(stage):
        for stream in range(2):
            for _, recv in w_copies(stream, stage):
                recv.wait_recv()

    def halo(step):
        cur = snaps.at[step]
        rows = CX * CY
        faces = [
            (cur.at[pl.ds(rows - CY, CY)], hx.at[step, 0], sides[0][0]),
            (cur.at[pl.ds(0, CY)], hx.at[step, 1], sides[0][1]),
            (hy_out.at[step, 0], hy.at[step, 0], sides[1][0]),
            (hy_out.at[step, 1], hy.at[step, 1], sides[1][1]),
            (cur.at[:, pl.ds(PEN - 128, 128)], hz.at[step, 0], sides[2][0]),
            (cur.at[:, pl.ds(0, 128)], hz.at[step, 1], sides[2][1]),
        ]
        return [
            remote(s, d, halo_s.at[step, i], halo_r.at[step, i], dev)
            for i, (s, d, dev) in enumerate(faces)
        ]

    def halo_start(step):
        copies = halo(step)
        for i in (0, 1, 4, 5):
            copies[i].start()
        for i in range(CX):
            hy_out[step, 0, pl.ds(i, 1), :] = snaps[step, pl.ds(i * CY + CY - 1, 1), :]
            hy_out[step, 1, pl.ds(i, 1), :] = snaps[step, pl.ds(i * CY, 1), :]
        copies[2].start()
        copies[3].start()

    row_id = lax.broadcasted_iota(jnp.int32, (CY, PEN), 0)
    lane_id = lax.broadcasted_iota(jnp.int32, (CY, PEN), 1)

    def advance(step):
        for c in halo(step):
            c.wait_recv()

        def layer(i):
            if i < 0:
                return hx[step, 0]
            if i >= CX:
                return hx[step, 1]
            return snaps[step, pl.ds(i * CY, CY), :]

        for i in range(CX):
            u = layer(i)
            xp, xm = layer(i + 1), layer(i - 1)
            yp = jnp.where(row_id == CY - 1, hy[step, 1, pl.ds(i, 1), :], pltpu.roll(u, CY - 1, 0))
            ym = jnp.where(row_id == 0, hy[step, 0, pl.ds(i, 1), :], pltpu.roll(u, 1, 0))
            zhi = hz[step, 1, pl.ds(i * CY, CY), :][:, 0:1]
            zlo = hz[step, 0, pl.ds(i * CY, CY), :][:, 127:128]
            zp = jnp.where(lane_id == PEN - 1, zhi, pltpu.roll(u, PEN - 1, 1))
            zm = jnp.where(lane_id == 0, zlo, pltpu.roll(u, 1, 1))
            lap = (xp + xm) + (yp + ym) + (zp + zm) - 6.0 * u
            adv = vel_ref[0, i] * (xp - xm) + vel_ref[1, i] * (yp - ym) + vel_ref[2, i] * (zp - zm)
            new = u + TIME_STEP * (lap - 0.5 * adv - rate_ref[i] * u)
            if step == STEPS - 1:
                adv_ref[i] = new
            else:
                snaps[step + 1, pl.ds(i * CY, CY), :] = new

    hot = jnp.where(
        lax.broadcasted_iota(jnp.int32, (CX * CY, S), 0) == picks_ref[...], 1.0, 0.0
    ).astype(BF16)

    tb = log2(T)
    tbits = [(gx // (1 << b)) % 2 for b in range(tb)]
    x_order = list(range(tb - 1, -1, -1))

    def x_copies(half, stage):
        cols = pl.ds(half * PEN, PEN)
        done, cur = x_order[:stage], x_order[stage]
        dev = {"gx": gx + (1 - 2 * tbits[cur]) * (1 << cur)}
        out = []
        for k in range(1 << stage):
            c = sum(tbits[b] * (1 << b) for b in range(tb) if b not in done)
            c = c + sum(((k >> j) & 1) * (1 << b) for j, b in enumerate(done))
            theirs = c + (1 - 2 * tbits[cur]) * (1 << cur)
            slot = (1 << stage) - 1 + k
            sems = (x_s.at[half, slot], x_r.at[half, slot])
            send = remote(xin.at[c, :, cols], xin.at[c, :, cols], *sems, dev)
            recv = remote(xin.at[theirs, :, cols], xin.at[theirs, :, cols], *sems, dev)
            out.append((send, recv))
        return out

    def x_start(half, stage):
        for send, _ in x_copies(half, stage):
            send.start()

    def x_wait(half, stage):
        for _, recv in x_copies(half, stage):
            recv.wait_recv()

    def x_send(half):
        xin[gx, :, pl.ds(half * PEN, PEN)] = mm(hot, snaps[half + 1].astype(BF16), TN).astype(BF16)
        x_start(half, 0)

    halo_start(0)
    own_in.wait()
    own_out.wait()
    w_start(0)
    w_stage = 0
    for step in range(STEPS):
        advance(step)
        if step < STEPS - 1:
            halo_start(step + 1)
            x_send(step)
        if step > 0:
            x_wait(0, step - 1)
            if step < tb:
                x_start(0, step)
        if w_stage < nb - 1:
            w_wait(w_stage)
            w_stage += 1
            w_start(w_stage)
    while True:
        w_wait(w_stage)
        w_stage += 1
        if w_stage == nb:
            break
        w_start(w_stage)
    x_wait(1, 0)
    if tb > 1:
        x_start(1, 1)
    for stage in range(STEPS - 1, tb):
        x_wait(0, stage)
        if stage + 1 < tb:
            x_start(0, stage + 1)
    snap3 = adv_ref[...].reshape(CX * CY, PEN)
    hi = snap3.astype(BF16)
    rest = snap3 - hi.astype(F32)
    mid = rest.astype(BF16)
    low = (rest - mid.astype(F32)).astype(BF16)
    target = (mm(hot, hi, TN) + mm(hot, mid, TN)) + mm(hot, low, TN)

    cb = 4 if D % 4 == 0 else D
    SA = T * S

    def half_product(rows, half):
        cols = pl.ds(half * PEN, PEN)
        return mm(win[rows, :, cols].reshape(cb * Hc, PEN), xin[:, :, cols].reshape(SA, PEN), NT)

    @pl.loop(0, D // cb)
    def _(b):
        rows = pl.ds(b * cb, cb)
        pre[rows] = half_product(rows, 0).reshape(cb, Hc, SA)

    for stage in range(1, tb):
        x_wait(1, stage)
        if stage + 1 < tb:
            x_start(1, stage + 1)

    @pl.loop(0, D // cb)
    def _(b):
        rows = pl.ds(b * cb, cb)
        v = pre[rows].reshape(cb * Hc, SA) + half_product(rows, 1)
        pre[rows] = v.reshape(cb, Hc, SA)
        hid[rows] = (v / (1.0 + jnp.exp(-v))).astype(BF16).reshape(cb, Hc, SA)

    def predict(t):
        h = hid[:, :, pl.ds(pl.multiple_of(t * S, S), S)].reshape(D * Hc, S)
        return mm(h, wout[...].reshape(D * Hc, PEN), TN)

    HP = PEN // 2

    def p_copy(h, k):
        return remote(part.at[h, k], prv.at[h, k], p_s.at[h, k], p_r.at[h, k], peers[k])

    for k in range(T - 1):
        val = predict((gx + 1 + k) % T)
        for h in range(2):
            part[h, k] = val[:, h * HP:(h + 1) * HP]
        p_copy(0, k).start()
    for k in range(T - 1):
        p_copy(1, k).start()
    total = predict(gx) - target

    def q_copy(h, k):
        src = (gx + T - 1 - k) % T
        cols = pl.ds(h * HP, HP)
        sems = (q_s.at[h, k], q_r.at[h, k])
        send = remote(res.at[gx, :, cols], res.at[gx, :, cols], *sems, peers[k])
        recv = remote(res.at[src, :, cols], res.at[src, :, cols], *sems, peers[k])
        return send, recv

    for h in range(2):
        val = total[:, h * HP:(h + 1) * HP]
        for k in range(T - 1):
            p_copy(h, k).wait_recv()
            val = val + prv[h, k]
        res[gx, :, pl.ds(h * HP, HP)] = (val * scale).astype(BF16)
        for k in range(T - 1):
            q_copy(h, k)[0].start()

    orders = [[0] + list(range(1, nb)), [0] + list(range(nb - 1, 0, -1))]
    offs = [sum(D >> (j + 1) for j in range(s)) for s in range(nb)]

    def g_slot(stage, vals):
        return offs[stage] + sum(v * (1 << j) for j, v in enumerate(vals))

    def g_copy(stream, stage, vals):
        order = orders[stream % 2]
        cur = order[stage]
        c = sum(mb[b] * (1 << b) for b in order[:stage]) + (1 - mb[cur]) * (1 << cur)
        c = c + sum(v * (1 << b) for v, b in zip(vals, order[stage + 1:]))
        slot = g_slot(stage, vals)
        keep = c + (2 * mb[cur] - 1) * (1 << cur)
        copy = remote(
            g.at[stream, c], rbuf.at[stream, slot], g_s.at[stream, slot], g_r.at[stream, slot],
            partner(cur),
        )
        return copy, slot, keep

    def patterns(n):
        return [[(k >> j) & 1 for j in range(n)] for k in range(1 << n)]

    NI = IN // W

    def put(stream, b, val):
        g[stream, pl.ds(b * cb, cb)] = val.reshape(cb, Hc, W)
        rest_bits = orders[stream % 2][1:]
        for vals in patterns(nb - 1):
            low_c = sum(v * (1 << bb) for v, bb in zip(vals, rest_bits))
            if b * cb <= low_c < (b + 1) * cb:
                g_copy(stream, 0, vals)[0].start()

    def reduce(stream, stage):
        order = orders[stream % 2]
        n = nb - 1 - stage
        if n == 0:
            copy, slot, keep = g_copy(stream, stage, [])
            copy.wait_recv()
            val = g[stream, keep] + rbuf[stream, slot]
            if stream < NI:
                gin_ref[:, pl.ds(stream * W, W)] = val
            else:
                gout_ref[:, pl.ds(stream * W - IN, W)] = val
            return
        nxt = mb[order[stage + 1]]
        for flip in (1, 0):
            bit = 1 - nxt if flip else nxt
            for vals in patterns(n - 1):
                copy, slot, keep = g_copy(stream, stage, [bit] + vals)
                copy.wait_recv()
                g[stream, keep] = g[stream, keep] + rbuf[stream, slot]
                if flip:
                    g_copy(stream, stage + 1, vals)[0].start()

    for h in range(2):
        for k in range(T - 1):
            q_copy(h, k)[1].wait_recv()
        for stream in range(NI, NS):
            if (stream - NI) * W // HP == h:
                r = res[:, :, pl.ds(stream * W - IN, W)].reshape(SA, W)
                for b in range(D // cb):
                    put(stream, b, mm(hid[pl.ds(b * cb, cb)].reshape(cb * Hc, SA), r))
    for b in range(D // cb):
        rows = pl.ds(b * cb, cb)
        back = mm(wout[rows].reshape(cb * Hc, PEN), res[...].reshape(SA, PEN), NT)
        dpre = (back * dsilu(pre[rows].reshape(cb * Hc, SA))).astype(BF16)
        if b == 0:
            for stream in range(NI, NS):
                reduce(stream, 0)
        for stream in range(NI):
            x = xin[:, :, pl.ds(stream * W, W)].reshape(SA, W)
            put(stream, b, mm(dpre, x))
    for stage in range(nb):
        for stream in list(range(NI, NS)) + list(range(NI)):
            if stage > 0 or stream < NI:
                reduce(stream, stage)

    for step in range(STEPS):
        for c in halo(step):
            c.wait_send()
    for stream in range(2):
        for stage in range(nb):
            for send, _ in w_copies(stream, stage):
                send.wait_send()
    for half in range(2):
        for stage in range(tb):
            for send, _ in x_copies(half, stage):
                send.wait_send()
        for k in range(T - 1):
            p_copy(half, k).wait_send()
            q_copy(half, k)[0].wait_send()
    for stream in range(NS):
        for stage in range(nb):
            for vals in patterns(nb - 1 - stage):
                g_copy(stream, stage, vals)[0].wait_send()


def shards(sizes, scalar_field, velocity, reaction_rate, sample_cells, weight_in, weight_out):
    T, NY, NZ = sizes
    D = NY * NZ
    nb = log2(D)
    CX, CY, PEN = scalar_field.shape
    S = sample_cells.shape[-1]
    Hc, IN = weight_in.shape
    SA = T * S
    W = PEN // SPLIT
    NS = (IN + PEN) // W
    scale = 1.0 / math.sqrt(S * T * D)
    rows = CX * CY
    dma = pltpu.SemaphoreType.DMA
    vmem = pl.BlockSpec(memory_space=pltpu.VMEM)
    return tuple(pl.pallas_call(
        functools.partial(kernel, sizes, scale),
        out_shape=(
            jax.ShapeDtypeStruct((CX, CY, PEN), F32),
            jax.ShapeDtypeStruct((Hc, IN), F32),
            jax.ShapeDtypeStruct((Hc, PEN), F32),
        ),
        in_specs=[vmem] * 6,
        out_specs=(vmem,) * 3,
        scratch_shapes=[
            pltpu.VMEM((STEPS, rows, PEN), F32),
            pltpu.VMEM((STEPS, 2, CY, PEN), F32),
            pltpu.VMEM((STEPS, 2, CX, PEN), F32),
            pltpu.VMEM((STEPS, 2, CX, PEN), F32),
            pltpu.VMEM((STEPS, 2, rows, 128), F32),
            pltpu.VMEM((T, S, IN), BF16),
            pltpu.VMEM((D, Hc, IN), BF16),
            pltpu.VMEM((D, Hc, PEN), BF16),
            pltpu.VMEM((D, Hc, SA), F32),
            pltpu.VMEM((D, Hc, SA), BF16),
            pltpu.VMEM((2, T - 1, S, PEN // 2), F32),
            pltpu.VMEM((2, T - 1, S, PEN // 2), F32),
            pltpu.VMEM((T, S, PEN), BF16),
            pltpu.VMEM((NS, D, Hc, W), F32),
            pltpu.VMEM((NS, D - 1, Hc, W), F32),
            dma((STEPS, 6)), dma((STEPS, 6)),
            dma((2, T - 1)), dma((2, T - 1)),
            dma((2, D - 1)), dma((2, D - 1)),
            dma((2, T - 1)), dma((2, T - 1)),
            dma((2, T - 1)), dma((2, T - 1)),
            dma((NS, D - 1)), dma((NS, D - 1)),
            dma((3,)),
        ],
        compiler_params=pltpu.CompilerParams(
            collective_id=0, has_side_effects=True, vmem_limit_bytes=60 * 1024 * 1024
        ),
    )(
        scalar_field.reshape(rows, PEN), velocity, reaction_rate,
        sample_cells.reshape(1, S), weight_in, weight_out,
    ))


def solution(mesh):
    sizes = (mesh.shape["gx"], mesh.shape["gy"], mesh.shape["gz"])
    in_specs = (
        P("gx", "gy", "gz"),
        P(None, "gx", "gy", "gz"),
        P("gx", "gy", "gz"),
        P("gx", "gy", "gz"),
        P(("gx", "gy", "gz"), None),
        P(("gx", "gy", "gz"), None),
    )
    out_specs = (P("gx", "gy", "gz"), P(("gx", "gy", "gz"), None), P(("gx", "gy", "gz"), None))
    return jax.shard_map(
        functools.partial(shards, sizes), mesh=mesh, in_specs=in_specs, out_specs=out_specs,
        check_vma=False,
    )
```
